32 devices in a mesh: grp: 2 (over x), orient: 16 (over z, y, core).
Axes of the slice: x: 2, y: 2, z: 4, core: 2. Of those that a mesh axis runs over, the one named last changes fastest.
Arguments:
- particles: bfloat16 [2048, 2048], P(('grp', 'orient')), parts along dimension 0, may hold values from -50 to 50
- references: bfloat16 [4096, 2048], P(('grp', 'orient')), parts along dimension 0, may hold values from -4 to 4
- tile_blocks: int32 [32, 6], P('grp'), parts along dimension 0, may hold values from 0 to 7, as said below
- tile_count: int32 [32], P('grp'), parts along dimension 0, may hold values from 1 to 6
- shift_start: int32 [32, 6], P('grp'), parts along dimension 0, may hold values from 1 to 16
Outputs:
- ref_update: float32 [4096, 2048], P(('grp', 'orient')), parts along dimension 0
- weight_sum: float32 [4096], P(('grp', 'orient')), parts along dimension 0
- log_evidence: float32 [2048], P(('grp', 'orient')), parts along dimension 0
The draws below stay inside these ranges and needn't reach their ends.
There are 2 independent parts, one for each index of `grp`. The reference program is written for one: setup_inputs(seed, part) draws one part's arguments, and reference() takes and returns one part's arrays. A program takes and returns all parts, laid end to end along the dimension named above; each array names one. Nothing has to cross between parts.
Inputs may be any that keep to these rules, and one draw needn't show every extreme that they name: `tile_blocks`: in each row the first tile_count entries are distinct particle blocks, and every particle block appears among the used entries of some row.
All inputs are finite; a program needn't handle non-finite values.
Results may differ from the reference program's by a relative error of at most 0.0033.
Values may be sent and summed in bfloat16 or wider, within the bound.
A program may use at most 128 MiB of HBM per device.

```python
import math
import jax
import jax.numpy as jnp
from jax import lax

K = 2048
NSH = 16
TILE = 128
MOST = 6
P_SIZE = 1024
O = 2048


def tile_lists(key):
    list_key = jax.random.fold_in(key, 11)
    count_key, offset_key, order_key, forced_key = jax.random.split(list_key, 4)
    column_total = O // TILE
    block_total = P_SIZE // TILE
    level_draw = jax.random.randint(count_key, (column_total,), 0, 6)
    counts = 1 + level_draw * level_draw // 6
    forced = jax.random.randint(forced_key, (), 0, column_total)
    column_ids = jnp.arange(column_total, dtype=jnp.int32)
    counts = jnp.where(column_ids == forced, MOST, counts)
    counts = jnp.where(column_ids == (forced + 1) % column_total, 1, counts)
    block_offset = jax.random.randint(offset_key, (), 0, block_total)
    first_slot = (column_ids + block_offset) % block_total
    random_scores = jax.random.randint(order_key, (column_total, block_total - 1), 0, 2 ** 30)
    shuffled = jnp.argsort(random_scores, axis=1).astype(jnp.int32)
    slot_offsets = shuffled[:, :MOST - 1] + 1
    later_slots = (first_slot[:, None] + slot_offsets) % block_total
    block_table = jnp.concatenate([first_slot[:, None], later_slots], axis=1).astype(jnp.int32)
    return (block_table, counts.astype(jnp.int32))


def ref_values(key):
    value_key = jax.random.fold_in(key, 23)
    return jnp.clip(jax.random.normal(value_key, (O, K), jnp.float32), -4.0, 4.0)


def draw_tile_blocks(key, part):
    return tile_lists(key)[0]


def draw_tile_count(key, part):
    return tile_lists(key)[1]


def draw_references(key, part):
    return ref_values(key).astype(jnp.bfloat16)


def draw_particles(key, part):
    image_key = jax.random.fold_in(key, 37)
    noise_key = jax.random.fold_in(image_key, 0)
    noise_values = jnp.clip(jax.random.normal(noise_key, (P_SIZE, K), jnp.float32), -4.0, 4.0)
    background = noise_values
    refs_all = ref_values(key)
    block_table, counts = tile_lists(key)
    block_total = P_SIZE // TILE
    slot_used = jnp.arange(MOST, dtype=jnp.int32)[None, :] < counts[:, None]
    membership = jnp.any((block_table[:, :, None] == jnp.arange(block_total, dtype=jnp.int32)[None, None, :]) & slot_used[:, :, None], axis=1)
    first_column = jnp.argmax(membership.astype(jnp.int32), axis=0).astype(jnp.int32)
    particle_ids = jnp.arange(P_SIZE, dtype=jnp.int32)
    particle_block = particle_ids % block_total
    member_index = particle_ids // block_total
    aligned_orient = first_column[particle_block] * TILE + member_index * 7 % TILE
    level = (2 + member_index // 16 % 3).astype(jnp.float32)
    strength = level * 48.0 / jnp.sqrt(jnp.float32(K))
    aligned = strength[:, None] * refs_all[aligned_orient] + 0.3 * noise_values
    result_values = jnp.where((member_index % 16 == 0)[:, None], aligned, background)
    return result_values.astype(jnp.bfloat16)


def set_ends(array, rng, least, largest):
    longest = array.shape.index(max(array.shape))
    spots = []
    for shift in (0, 1):
        where = [jax.random.randint(jax.random.fold_in(rng, axis), (), 0, length) for axis, length in enumerate(array.shape)]
        where[longest] = (where[longest] + shift) % array.shape[longest]
        spots.append(tuple(where))
    return array.at[spots[0]].set(least).at[spots[1]].set(largest)


def setup_inputs(seed: int = 0, part: int = 0) -> dict:
    key_of = jax.random.split(jax.random.key(seed), 6)
    part_splits = jax.random.split(jax.random.fold_in(key_of[5], part), 6)
    particles = draw_particles(jax.random.fold_in(jax.random.fold_in(key_of[5], part), 71), part)
    references = draw_references(jax.random.fold_in(jax.random.fold_in(key_of[5], part), 71), part)
    tile_blocks = draw_tile_blocks(jax.random.fold_in(jax.random.fold_in(key_of[5], part), 71), part)
    tile_count = draw_tile_count(jax.random.fold_in(jax.random.fold_in(key_of[5], part), 71), part)
    shift_start = set_ends(jax.random.randint(part_splits[4], (O // TILE, MOST), 1, 17), jax.random.fold_in(part_splits[4], 1), 1, 16).astype(jnp.int32)
    return {"particles": particles, "references": references, "tile_blocks": tile_blocks, "tile_count": tile_count, "shift_start": shift_start}


very_negative = -1e+30

def shift_phases(window_start):
    half_width = K // 2
    freq_index = jnp.arange(half_width, dtype=jnp.int32)
    freq_x = (freq_index % 32).astype(jnp.float32)
    freq_y = (freq_index // 32 - K // 128).astype(jnp.float32)
    grid_index = window_start + jnp.arange(NSH, dtype=jnp.int32)
    delta_x = (grid_index - 16).astype(jnp.float32) * 0.5
    delta_y = (5 * grid_index % 7 - 3).astype(jnp.float32) * 0.5
    angles = 2.0 * math.pi / 64.0 * (delta_x[:, None] * freq_x[None, :] + delta_y[:, None] * freq_y[None, :])
    return (jnp.cos(angles), jnp.sin(angles))

def shifted_images(image_block, window_start):
    cosine_table, sine_table = shift_phases(window_start)
    half_width = K // 2
    real_part = image_block[:, :half_width].astype(jnp.float32)[None]
    imag_part = image_block[:, half_width:].astype(jnp.float32)[None]
    new_real = real_part * cosine_table[:, None, :] - imag_part * sine_table[:, None, :]
    new_imag = real_part * sine_table[:, None, :] + imag_part * cosine_table[:, None, :]
    stacked = jnp.concatenate([new_real, new_imag], axis=2).astype(jnp.bfloat16)
    return stacked.reshape(NSH * image_block.shape[0], K)

def tile_scores(shifted, ref_block, ref_norms):
    products = lax.dot_general(shifted, ref_block, (((1,), (1,)), ((), ())), preferred_element_type=jnp.float32)
    return (products - 0.5 * ref_norms[None, :]) / math.sqrt(K)

def reference(particles, references, tile_blocks, tile_count, shift_start):
    column_total = references.shape[0] // TILE
    particle_total = particles.shape[0]
    block_total = particle_total // TILE
    by_block = particles.reshape(TILE, block_total, K)
    ref_norms_all = lax.optimization_barrier(jnp.sum(references.astype(jnp.float32) ** 2, axis=1))
    item_total = column_total * MOST
    item_ids = jnp.arange(item_total, dtype=jnp.int32)

    def item_parts(item_index):
        column = item_index // MOST
        slot_index = item_index % MOST
        active = slot_index < tile_count[column]
        block_id = tile_blocks[column, slot_index].astype(jnp.int32)
        return (column, slot_index, active, block_id)

    def make_shifted(column, slot_index, block_id):
        image_block = lax.dynamic_index_in_dim(by_block, block_id, 1, keepdims=False)
        return shifted_images(image_block, shift_start[column, slot_index])

    def score_item(item_index):
        column, slot_index, active, block_id = item_parts(item_index)

        def compute(unused):
            shifted = make_shifted(column, slot_index, block_id)
            ref_block = lax.dynamic_slice_in_dim(references, (column * TILE).astype(jnp.int32), TILE, 0)
            norms = lax.dynamic_slice_in_dim(ref_norms_all, (column * TILE).astype(jnp.int32), TILE, 0)
            return tile_scores(shifted, ref_block, norms)

        def skipped(unused):
            return jnp.full((NSH * TILE, TILE), very_negative, jnp.float32)
        return lax.cond(active, compute, skipped, 0)
    scores = lax.map(score_item, item_ids)
    row_index = (tile_blocks.reshape(-1)[:, None] + block_total * jnp.arange(TILE, dtype=jnp.int32)[None, :]).astype(jnp.int32)
    by_particle = scores.reshape(item_total, NSH, TILE, TILE)
    item_top = lax.optimization_barrier(jnp.max(by_particle, axis=(1, 3)))
    top = jnp.full((particle_total,), very_negative, jnp.float32).at[row_index.reshape(-1)].max(item_top.reshape(-1))
    item_sum = lax.optimization_barrier(jnp.sum(jnp.exp(by_particle - top[row_index][:, None, :, None]), axis=(1, 3)))
    total = jnp.zeros((particle_total,), jnp.float32).at[row_index.reshape(-1)].add(item_sum.reshape(-1))
    log_evidence = top + jnp.log(total)
    top_grid = top.reshape(TILE, block_total)
    total_grid = total.reshape(TILE, block_total)

    def back_item(item_index):
        column, slot_index, active, block_id = item_parts(item_index)

        def compute(unused):
            shifted = make_shifted(column, slot_index, block_id)
            particle_top = lax.dynamic_index_in_dim(top_grid, block_id, 1, keepdims=False)
            particle_sum = lax.dynamic_index_in_dim(total_grid, block_id, 1, keepdims=False)
            item_scores = scores[item_index].reshape(NSH, TILE, TILE)
            weights = (jnp.exp(item_scores - particle_top[None, :, None]) / particle_sum[None, :, None]).astype(jnp.bfloat16)
            weights = weights.reshape(NSH * TILE, TILE)
            update = lax.dot_general(weights, shifted, (((0,), (0,)), ((), ())), preferred_element_type=jnp.float32)
            return (update, lax.optimization_barrier(jnp.sum(weights.astype(jnp.float32), axis=0)))

        def skipped(unused):
            return (jnp.zeros((TILE, K), jnp.float32), jnp.zeros((TILE,), jnp.float32))
        return lax.cond(active, compute, skipped, 0)
    updates, weight_totals = lax.map(back_item, item_ids)
    ref_update = lax.optimization_barrier(jnp.sum(updates.reshape(column_total, MOST, TILE, K), axis=1)).reshape(column_total * TILE, K)
    weight_sum = lax.optimization_barrier(jnp.sum(weight_totals.reshape(column_total, MOST, TILE), axis=1)).reshape(column_total * TILE)
    return (ref_update, weight_sum, log_evidence)
```

```python
import functools
import math

import jax
import jax.numpy as jnp
from jax import lax
from jax.experimental import pallas as pl
from jax.experimental.pallas import tpu as pltpu
from jax.sharding import PartitionSpec as P

K = 2048
NSH = 16
TILE = 128
GRID = 2 * NSH
CHUNK = 4

very_negative = -1e30


def phase_tables():
    half_width = K // 2
    freq_index = jnp.arange(half_width, dtype=jnp.int32)
    freq_x = (freq_index % 32).astype(jnp.float32)
    freq_y = (freq_index // 32 - K // 128).astype(jnp.float32)
    grid_index = jnp.arange(GRID, dtype=jnp.int32)
    delta_x = (grid_index - 16).astype(jnp.float32) * 0.5
    delta_y = (5 * grid_index % 7 - 3).astype(jnp.float32) * 0.5
    angles = (
        2.0
        * math.pi
        / 64.0
        * (delta_x[:, None] * freq_x[None, :] + delta_y[:, None] * freq_y[None, :])
    )
    return jnp.cos(angles), jnp.sin(angles)


def score_kernel(
    blocks, starts, count, images, refs, norms, cos_ref, sin_ref,
    shifted, scores, tops, sums, best,
):
    slot, part = pl.program_id(0), pl.program_id(1)
    half = K // 2

    @pl.when((slot == 0) & (part == 0))
    def _():
        tops[...] = jnp.full_like(tops, very_negative)
        sums[...] = jnp.zeros_like(sums)

    @pl.when(slot < count[0])
    def _():
        for t in range(CHUNK):
            g = starts[slot] + part * CHUNK + t
            image = images[...].astype(jnp.float32).reshape(TILE, K)
            real, imag = image[:, :half], image[:, half:]
            c = cos_ref[pl.ds(g, 1), :]
            s = sin_ref[pl.ds(g, 1), :]
            rows = pl.ds(t * TILE, TILE)
            shifted[rows, :half] = (real * c - imag * s).astype(jnp.bfloat16)
            shifted[rows, half:] = (real * s + imag * c).astype(jnp.bfloat16)
        products = lax.dot_general(
            shifted[...], refs[...], (((1,), (1,)), ((), ())),
            preferred_element_type=jnp.float32,
        )
        values = (products - 0.5 * norms[...]) * (1.0 / math.sqrt(K))
        scores[part] = values
        tallest = jnp.max(values.reshape(CHUNK, TILE, TILE), axis=0)

        @pl.when(part == 0)
        def _():
            best[...] = tallest

        @pl.when(part > 0)
        def _():
            best[...] = jnp.maximum(best[...], tallest)

        @pl.when(part == NSH // CHUNK - 1)
        def _():
            top = jnp.max(best[...], axis=1, keepdims=True)
            total = jnp.zeros((TILE, TILE), jnp.float32)
            for q in range(NSH // CHUNK):
                for t in range(CHUNK):
                    total += jnp.exp(scores[q, pl.ds(t * TILE, TILE), :] - top)
            total = jnp.sum(total, axis=1, keepdims=True)
            lane = lax.broadcasted_iota(jnp.int32, tops.shape, 1)
            mine = lane == blocks[slot]
            tops[...] = jnp.where(mine, top, tops[...])
            sums[...] = jnp.where(mine, total, sums[...])


def update_kernel(blocks, count, shifted, scores, tops, sums, update, mass):
    slot, part = pl.program_id(0), pl.program_id(1)

    @pl.when((slot == 0) & (part == 0))
    def _():
        update[...] = jnp.zeros_like(update)
        mass[...] = jnp.zeros_like(mass)

    @pl.when(slot < count[0])
    def _():
        lane = lax.broadcasted_iota(jnp.int32, tops.shape, 1)
        mine = lane == blocks[slot]
        top = jnp.sum(jnp.where(mine, tops[...], 0.0), axis=1, keepdims=True)
        total = jnp.sum(jnp.where(mine, sums[...], 0.0), axis=1, keepdims=True)
        values = scores[...].reshape(CHUNK, TILE, TILE)
        weights = (jnp.exp(values - top[None]) / total[None]).astype(jnp.bfloat16)
        weights = weights.reshape(CHUNK * TILE, TILE)
        mass[...] += jnp.sum(weights.astype(jnp.float32), axis=0, keepdims=True)
        update[...] += lax.dot_general(
            weights, shifted[...], (((0,), (0,)), ((), ())),
            preferred_element_type=jnp.float32,
        )


def body(particles, references, tile_blocks, tile_count, shift_start):
    local_rows = particles.shape[0]
    axis_count = lax.axis_size("orient")
    my_index = lax.axis_index("orient")
    total_rows = local_rows * axis_count
    block_total = total_rows // TILE
    most = tile_blocks.shape[1]
    parts = NSH // CHUNK
    per = local_rows // block_total
    count = tile_count[my_index].reshape(1)
    blocks = tile_blocks[my_index]
    starts = shift_start[my_index]
    norms = jnp.sum(references.astype(jnp.float32) ** 2, axis=1)[None, :]
    cos_table, sin_table = phase_tables()

    turned = particles.reshape(per, block_total, K).transpose(1, 0, 2)
    by_block = lax.all_gather(turned, "orient", axis=0)
    if per % 8:
        by_block = by_block.transpose(1, 0, 2, 3).reshape(1, block_total, TILE, K)

    def held(slot, count):
        return jnp.minimum(slot, count[0] - 1)

    def held_part(slot, part, count):
        return jnp.where(slot < count[0], part, parts - 1)

    whole = lambda shape: pl.BlockSpec(shape, lambda s, p, *_: (0,) * len(shape))
    lead, _, deep, _ = by_block.shape
    shifted, scores, tops, sums = pl.pallas_call(
        score_kernel,
        grid_spec=pltpu.PrefetchScalarGridSpec(
            num_scalar_prefetch=3,
            grid=(most, parts),
            in_specs=[
                pl.BlockSpec(
                    (lead, None, deep, K),
                    lambda s, p, b, g, c: (0, b[held(s, c)], 0, 0),
                ),
                whole((TILE, K)),
                whole((1, TILE)),
                whole((GRID, K // 2)),
                whole((GRID, K // 2)),
            ],
            out_specs=[
                pl.BlockSpec(
                    (None, CHUNK * TILE, K),
                    lambda s, p, b, g, c: (held(s, c), held_part(s, p, c), 0),
                ),
                pl.BlockSpec(
                    (None, parts, CHUNK * TILE, TILE),
                    lambda s, p, b, g, c: (held(s, c), 0, 0, 0),
                ),
                whole((TILE, block_total)),
                whole((TILE, block_total)),
            ],
            scratch_shapes=[pltpu.VMEM((TILE, TILE), jnp.float32)],
        ),
        out_shape=[
            jax.ShapeDtypeStruct((most, NSH * TILE, K), jnp.bfloat16),
            jax.ShapeDtypeStruct((most, parts, CHUNK * TILE, TILE), jnp.float32),
            jax.ShapeDtypeStruct((TILE, block_total), jnp.float32),
            jax.ShapeDtypeStruct((TILE, block_total), jnp.float32),
        ],
        name="scores",
    )(blocks, starts, count, by_block, references, norms, cos_table, sin_table)

    pair = lax.all_gather(jnp.stack([tops, sums]), "orient", axis=0)
    global_top = jnp.max(pair[:, 0], axis=0)
    global_sum = jnp.sum(pair[:, 1] * jnp.exp(pair[:, 0] - global_top), axis=0)

    update, mass = pl.pallas_call(
        update_kernel,
        grid_spec=pltpu.PrefetchScalarGridSpec(
            num_scalar_prefetch=2,
            grid=(most, parts),
            in_specs=[
                pl.BlockSpec(
                    (None, CHUNK * TILE, K),
                    lambda s, p, b, c: (held(s, c), held_part(s, p, c), 0),
                ),
                pl.BlockSpec(
                    (None, None, CHUNK * TILE, TILE),
                    lambda s, p, b, c: (held(s, c), held_part(s, p, c), 0, 0),
                ),
                whole((TILE, block_total)),
                whole((TILE, block_total)),
            ],
            out_specs=[whole((TILE, K)), whole((1, TILE))],
        ),
        out_shape=[
            jax.ShapeDtypeStruct((TILE, K), jnp.float32),
            jax.ShapeDtypeStruct((1, TILE), jnp.float32),
        ],
        name="update",
    )(blocks, count, shifted, scores, global_top, global_sum)

    evidence = global_top + jnp.log(global_sum)
    mine = lax.dynamic_slice_in_dim(evidence, my_index * per, per, 0)
    return update, mass.reshape(TILE), mine.reshape(local_rows)


def solution(mesh):
    in_specs = (
        P(("grp", "orient"), None),
        P(("grp", "orient"), None),
        P("grp", None),
        P("grp"),
        P("grp", None),
    )
    out_specs = (P(("grp", "orient"), None), P(("grp", "orient")), P(("grp", "orient")))
    return jax.shard_map(body, mesh=mesh, in_specs=in_specs, out_specs=out_specs, check_vma=False)
```

```python
import functools
import math

import jax
import jax.numpy as jnp
from jax import lax
from jax.experimental import pallas as pl
from jax.experimental.pallas import tpu as pltpu
from jax.sharding import PartitionSpec as P

K = 2048
NSH = 16
TILE = 128
GRID = 2 * NSH
CHUNK = 4

very_negative = -1e30


def phase_tables():
    half_width = K // 2
    freq_index = jnp.arange(half_width, dtype=jnp.int32)
    freq_x = (freq_index % 32).astype(jnp.float32)
    freq_y = (freq_index // 32 - K // 128).astype(jnp.float32)
    grid_index = jnp.arange(GRID, dtype=jnp.int32)
    delta_x = (grid_index - 16).astype(jnp.float32) * 0.5
    delta_y = (5 * grid_index % 7 - 3).astype(jnp.float32) * 0.5
    angles = (
        2.0
        * math.pi
        / 64.0
        * (delta_x[:, None] * freq_x[None, :] + delta_y[:, None] * freq_y[None, :])
    )
    return jnp.cos(angles), jnp.sin(angles)


def remote(src, dst, send, recv, target):
    return pltpu.make_async_remote_copy(
        src_ref=src,
        dst_ref=dst,
        send_sem=send,
        recv_sem=recv,
        device_id={"orient": target},
        device_id_type=pl.DeviceIdType.MESH,
    )


def greet(neighbours):
    barrier = pltpu.get_barrier_semaphore()
    arrivals = 0
    for target, present in neighbours:

        @pl.when(present)
        def _():
            pl.semaphore_signal(
                barrier, inc=1, device_id={"orient": target},
                device_id_type=pl.DeviceIdType.MESH,
            )

        arrivals = arrivals + jnp.where(present, 1, 0)
    pl.semaphore_wait(barrier, arrivals)


def gather_kernel(
    depth, width, mine, refs, out, norms, up_sem, down_sem, side_sem, twin_sem, recv_sem, own_sem
):
    me = lax.axis_index("orient")
    core = lax.rem(me, 2)
    chip = me // 2
    z, y = chip // width, lax.rem(chip, width)

    def at(zz, yy, cc):
        return (zz * width + yy) * 2 + cc

    up, down, twin = at(z + 1, y, core), at(z - 1, y, core), at(z, y, 1 - core)
    sides = [lax.rem(y + k, width) for k in range(1, width)]
    has_up, has_down = z < depth - 1, z > 0
    greet(
        [(up, has_up), (down, has_down), (twin, me >= 0)]
        + [(at(z, other, core), me >= 0) for other in sides]
    )

    def outgoing(idx, src, kind, k=0):
        send, target = dict(
            up=(up_sem, up),
            down=(down_sem, down),
            twin=(twin_sem, twin),
            side=(side_sem.at[k], at(z, sides[k], core) if sides else me),
        )[kind]
        return remote(src, out.at[idx], send.at[idx], recv_sem.at[idx], target)

    def arrived(idx):
        outgoing(idx, out.at[idx], "twin").wait_recv()

    pl.when(has_up)(lambda: outgoing(me, mine, "up").start())
    pl.when(has_down)(lambda: outgoing(me, mine, "down").start())
    for k in range(len(sides)):
        outgoing(me, mine, "side", k).start()
    outgoing(me, mine, "twin").start()
    keep = pltpu.make_async_copy(mine, out.at[me], own_sem)
    keep.start()

    folded = jnp.zeros((TILE, 128), jnp.float32)
    for k in range(K // 128):
        piece = refs[:, pl.ds(k * 128, 128)].astype(jnp.float32)
        folded += piece * piece
    norms[...] = jnp.sum(folded.T, axis=0, keepdims=True)

    def from_line(zz, onward, has_onward):
        idx = at(zz, y, core)
        arrived(idx)
        pl.when(has_onward)(lambda: outgoing(idx, out.at[idx], onward).start())
        for k in range(len(sides)):
            outgoing(idx, out.at[idx], "side", k).start()
        outgoing(idx, out.at[idx], "twin").start()

    def from_side(zz):
        for other in sides:
            idx = at(zz, other, core)
            arrived(idx)
            outgoing(idx, out.at[idx], "twin").start()

    for d in range(1, depth + 1):
        if d < depth:
            pl.when(z - d >= 0)(functools.partial(from_line, z - d, "up", has_up))
            pl.when(z + d < depth)(functools.partial(from_line, z + d, "down", has_down))
        if d == 1:
            from_side(z)
        else:
            pl.when(z - d + 1 >= 0)(functools.partial(from_side, z - d + 1))
            pl.when(z + d - 1 < depth)(functools.partial(from_side, z + d - 1))

    for zz in range(depth):
        for yy in range(width):
            arrived(at(zz, yy, 1 - core))

    keep.wait()
    for zz in range(depth):
        idx = at(zz, y, core)
        pl.when(has_up & (zz <= z))(lambda: outgoing(idx, mine, "up").wait_send())
        pl.when(has_down & (zz >= z))(lambda: outgoing(idx, mine, "down").wait_send())
        for k in range(len(sides)):
            outgoing(idx, mine, "side", k).wait_send()
        for yy in range(width):
            outgoing(at(zz, yy, core), mine, "twin").wait_send()


def gather_blocks(turned, references, width):
    count = lax.axis_size("orient")
    depth = count // (2 * width)
    return pl.pallas_call(
        functools.partial(gather_kernel, depth, width),
        in_specs=[pl.BlockSpec(memory_space=pltpu.VMEM)] * 2,
        out_specs=[pl.BlockSpec(memory_space=pl.ANY), pl.BlockSpec(memory_space=pltpu.VMEM)],
        out_shape=[
            jax.ShapeDtypeStruct((count,) + turned.shape, turned.dtype),
            jax.ShapeDtypeStruct((1, TILE), jnp.float32),
        ],
        scratch_shapes=[
            pltpu.SemaphoreType.DMA((count,)),
            pltpu.SemaphoreType.DMA((count,)),
            pltpu.SemaphoreType.DMA((max(width - 1, 1), count)),
            pltpu.SemaphoreType.DMA((count,)),
            pltpu.SemaphoreType.DMA((count,)),
            pltpu.SemaphoreType.DMA,
        ],
        compiler_params=pltpu.CompilerParams(collective_id=0, has_side_effects=True),
        name="gather",
    )(turned, references)


def merge_kernel(count, mine, top, total, evidence, landed, send_sem, recv_sem):
    me = lax.axis_index("orient")
    others = [lax.rem(me + k, count) for k in range(1, count)]
    greet([(other, me >= 0) for other in others])
    copies = [
        remote(mine, landed.at[k], send_sem.at[k], recv_sem.at[k], other)
        for k, other in enumerate(others)
    ]
    for copy in copies:
        copy.start()
    for copy in copies:
        copy.wait_recv()
    half = mine.shape[0] // 2
    best = mine[:half]
    for k in range(count - 1):
        best = jnp.maximum(best, landed[k, :half])
    joint = mine[half:] * jnp.exp(mine[:half] - best)
    for k in range(count - 1):
        joint += landed[k, half:] * jnp.exp(landed[k, :half] - best)
    top[...] = best
    total[...] = joint
    evidence[...] = best + jnp.log(joint)
    for copy in copies:
        copy.wait_send()


def merge_stats(stats):
    count = lax.axis_size("orient")
    half = jax.ShapeDtypeStruct((stats.shape[0] // 2, TILE), jnp.float32)
    vmem = pl.BlockSpec(memory_space=pltpu.VMEM)
    return pl.pallas_call(
        functools.partial(merge_kernel, count),
        in_specs=[vmem],
        out_specs=[vmem] * 3,
        out_shape=[half] * 3,
        scratch_shapes=[
            pltpu.VMEM((count - 1,) + stats.shape, jnp.float32),
            pltpu.SemaphoreType.DMA((count - 1,)),
            pltpu.SemaphoreType.DMA((count - 1,)),
        ],
        compiler_params=pltpu.CompilerParams(collective_id=1, has_side_effects=True),
        name="merge",
    )(stats)


def score_kernel(
    blocks, starts, count, images, refs, norms, cos_ref, sin_ref,
    shifted, scores, stats, best,
):
    slot, part = pl.program_id(0), pl.program_id(1)
    half = K // 2

    @pl.when((slot == 0) & (part == 0))
    def _():
        row = lax.broadcasted_iota(jnp.int32, stats.shape, 0)
        stats[...] = jnp.where(row < stats.shape[0] // 2, very_negative, 0.0)

    @pl.when(slot < count[0])
    def _():
        for t in range(CHUNK):
            g = starts[slot] + part * CHUNK + t
            image = images[...].astype(jnp.float32).reshape(TILE, K)
            real, imag = image[:, :half], image[:, half:]
            c = cos_ref[pl.ds(g, 1), :]
            s = sin_ref[pl.ds(g, 1), :]
            rows = pl.ds(t * TILE, TILE)
            shifted[rows, :half] = (real * c - imag * s).astype(jnp.bfloat16)
            shifted[rows, half:] = (real * s + imag * c).astype(jnp.bfloat16)
        products = lax.dot_general(
            shifted[...], refs[...], (((1,), (1,)), ((), ())),
            preferred_element_type=jnp.float32,
        )
        values = (products - 0.5 * norms[...]) * (1.0 / math.sqrt(K))
        scores[part] = values
        tallest = jnp.max(values.reshape(CHUNK, TILE, TILE), axis=0)

        @pl.when(part == 0)
        def _():
            best[...] = tallest

        @pl.when(part > 0)
        def _():
            best[...] = jnp.maximum(best[...], tallest)

        @pl.when(part == NSH // CHUNK - 1)
        def _():
            top = jnp.max(best[...], axis=1, keepdims=True)
            total = jnp.zeros((TILE, TILE), jnp.float32)
            for q in range(NSH // CHUNK):
                for t in range(CHUNK):
                    total += jnp.exp(scores[q, pl.ds(t * TILE, TILE), :] - top)
            block = blocks[slot]
            stats[pl.ds(block, 1), :] = jnp.max(best[...].T, axis=0, keepdims=True)
            stats[pl.ds(block + stats.shape[0] // 2, 1), :] = jnp.sum(
                total.T, axis=0, keepdims=True
            )


def update_kernel(blocks, count, shifted, scores, tops, sums, update, mass):
    slot, part = pl.program_id(0), pl.program_id(1)

    @pl.when((slot == 0) & (part == 0))
    def _():
        update[...] = jnp.zeros_like(update)
        mass[...] = jnp.zeros_like(mass)

    @pl.when(slot < count[0])
    def _():
        row = pl.ds(blocks[slot], 1)
        top = jnp.broadcast_to(tops[row, :], (TILE, TILE)).T
        total = jnp.broadcast_to(sums[row, :], (TILE, TILE)).T
        values = scores[...].reshape(CHUNK, TILE, TILE)
        weights = (jnp.exp(values - top[None]) / total[None]).astype(jnp.bfloat16)
        weights = weights.reshape(CHUNK * TILE, TILE)
        mass[...] += jnp.sum(weights.astype(jnp.float32), axis=0, keepdims=True)
        update[...] += lax.dot_general(
            weights, shifted[...], (((0,), (0,)), ((), ())),
            preferred_element_type=jnp.float32,
        )


def body(width, particles, references, tile_blocks, tile_count, shift_start):
    local_rows = particles.shape[0]
    axis_count = lax.axis_size("orient")
    my_index = lax.axis_index("orient")
    total_rows = local_rows * axis_count
    block_total = total_rows // TILE
    most = tile_blocks.shape[1]
    parts = NSH // CHUNK
    per = local_rows // block_total
    count = tile_count[my_index].reshape(1)
    blocks = tile_blocks[my_index]
    starts = shift_start[my_index]
    cos_table, sin_table = phase_tables()

    turned = particles.reshape(per, block_total, K).transpose(1, 0, 2)
    by_block, norms = gather_blocks(turned, references, width)
    if per % 8:
        by_block = by_block.transpose(1, 0, 2, 3).reshape(1, block_total, TILE, K)

    def held(slot, count):
        return jnp.minimum(slot, count[0] - 1)

    def held_part(slot, part, count):
        return jnp.where(slot < count[0], part, parts - 1)

    whole = lambda shape: pl.BlockSpec(shape, lambda s, p, *_: (0,) * len(shape))
    lead, _, deep, _ = by_block.shape
    shifted, scores, stats = pl.pallas_call(
        score_kernel,
        grid_spec=pltpu.PrefetchScalarGridSpec(
            num_scalar_prefetch=3,
            grid=(most, parts),
            in_specs=[
                pl.BlockSpec(
                    (lead, None, deep, K),
                    lambda s, p, b, g, c: (0, b[held(s, c)], 0, 0),
                ),
                whole((TILE, K)),
                whole((1, TILE)),
                whole((GRID, K // 2)),
                whole((GRID, K // 2)),
            ],
            out_specs=[
                pl.BlockSpec(
                    (None, CHUNK * TILE, K),
                    lambda s, p, b, g, c: (held(s, c), held_part(s, p, c), 0),
                ),
                pl.BlockSpec(
                    (None, parts, CHUNK * TILE, TILE),
                    lambda s, p, b, g, c: (held(s, c), 0, 0, 0),
                ),
                whole((2 * block_total, TILE)),
            ],
            scratch_shapes=[pltpu.VMEM((TILE, TILE), jnp.float32)],
        ),
        out_shape=[
            jax.ShapeDtypeStruct((most, NSH * TILE, K), jnp.bfloat16),
            jax.ShapeDtypeStruct((most, parts, CHUNK * TILE, TILE), jnp.float32),
            jax.ShapeDtypeStruct((2 * block_total, TILE), jnp.float32),
        ],
        name="scores",
    )(blocks, starts, count, by_block, references, norms, cos_table, sin_table)

    global_top, global_sum, evidence = merge_stats(stats)

    update, mass = pl.pallas_call(
        update_kernel,
        grid_spec=pltpu.PrefetchScalarGridSpec(
            num_scalar_prefetch=2,
            grid=(most, parts),
            in_specs=[
                pl.BlockSpec(
                    (None, CHUNK * TILE, K),
                    lambda s, p, b, c: (held(s, c), held_part(s, p, c), 0),
                ),
                pl.BlockSpec(
                    (None, None, CHUNK * TILE, TILE),
                    lambda s, p, b, c: (held(s, c), held_part(s, p, c), 0, 0),
                ),
                whole((block_total, TILE)),
                whole((block_total, TILE)),
            ],
            out_specs=[whole((TILE, K)), whole((1, TILE))],
        ),
        out_shape=[
            jax.ShapeDtypeStruct((TILE, K), jnp.float32),
            jax.ShapeDtypeStruct((1, TILE), jnp.float32),
        ],
        name="update",
    )(blocks, count, shifted, scores, global_top, global_sum)

    mine = lax.dynamic_slice_in_dim(evidence, my_index * per, per, 1)
    return update, mass.reshape(TILE), mine.T.reshape(local_rows)


def solution(mesh):
    in_specs = (
        P(("grp", "orient"), None),
        P(("grp", "orient"), None),
        P("grp", None),
        P("grp"),
        P("grp", None),
    )
    out_specs = (P(("grp", "orient"), None), P(("grp", "orient")), P(("grp", "orient")))
    width = max(1, 4 // mesh.shape["grp"])
    if mesh.shape["orient"] % (2 * width):
        width = 1
    return jax.shard_map(functools.partial(body, width), mesh=mesh, in_specs=in_specs, out_specs=out_specs, check_vma=False)
```

```python
import functools
import math

import jax
import jax.numpy as jnp
from jax import lax
from jax.experimental import pallas as pl
from jax.experimental.pallas import tpu as pltpu
from jax.sharding import PartitionSpec as P

K = 2048
NSH = 16
TILE = 128
GRID = 2 * NSH
SHIFTS = 16
MERGED = 4
FOLD = 16

very_negative = -1e30


def phase_tables():
    half_width = K // 2
    freq_index = jnp.arange(half_width, dtype=jnp.int32)
    freq_x = (freq_index % 32).astype(jnp.float32)
    freq_y = (freq_index // 32 - K // 128).astype(jnp.float32)
    grid_index = jnp.arange(GRID, dtype=jnp.int32)
    delta_x = (grid_index - 16).astype(jnp.float32) * 0.5
    delta_y = (5 * grid_index % 7 - 3).astype(jnp.float32) * 0.5
    angles = (
        2.0
        * math.pi
        / 64.0
        * (delta_x[:, None] * freq_x[None, :] + delta_y[:, None] * freq_y[None, :])
    )
    return jnp.cos(angles), jnp.sin(angles)


def remote(src, dst, send, recv, target):
    return pltpu.make_async_remote_copy(
        src_ref=src,
        dst_ref=dst,
        send_sem=send,
        recv_sem=recv,
        device_id={"orient": target},
        device_id_type=pl.DeviceIdType.MESH,
    )


def greet(neighbours):
    barrier = pltpu.get_barrier_semaphore()
    arrivals = 0
    for target, present in neighbours:

        @pl.when(present)
        def _():
            pl.semaphore_signal(
                barrier, inc=1, device_id={"orient": target},
                device_id_type=pl.DeviceIdType.MESH,
            )

        arrivals = arrivals + jnp.where(present, 1, 0)
    pl.semaphore_wait(barrier, arrivals)


def gather_kernel(
    depth, width, mine, refs, out, norms, up_sem, down_sem, side_sem, twin_sem, recv_sem, own_sem
):
    me = lax.axis_index("orient")
    core = lax.rem(me, 2)
    chip = me // 2
    z, y = chip // width, lax.rem(chip, width)

    def at(zz, yy, cc):
        return (zz * width + yy) * 2 + cc

    up, down, twin = at(z + 1, y, core), at(z - 1, y, core), at(z, y, 1 - core)
    sides = [lax.rem(y + k, width) for k in range(1, width)]
    has_up, has_down = z < depth - 1, z > 0
    greet(
        [(up, has_up), (down, has_down), (twin, me >= 0)]
        + [(at(z, other, core), me >= 0) for other in sides]
    )

    def outgoing(idx, src, kind, k=0):
        send, target = dict(
            up=(up_sem, up),
            down=(down_sem, down),
            twin=(twin_sem, twin),
            side=(side_sem.at[k], at(z, sides[k], core) if sides else me),
        )[kind]
        return remote(src, out.at[idx], send.at[idx], recv_sem.at[idx], target)

    def arrived(idx):
        outgoing(idx, out.at[idx], "twin").wait_recv()

    pl.when(has_up)(lambda: outgoing(me, mine, "up").start())
    pl.when(has_down)(lambda: outgoing(me, mine, "down").start())
    for k in range(len(sides)):
        outgoing(me, mine, "side", k).start()
    outgoing(me, mine, "twin").start()
    keep = pltpu.make_async_copy(mine, out.at[me], own_sem)
    keep.start()

    folded = jnp.zeros((TILE, 128), jnp.float32)
    for k in range(K // 128):
        piece = refs[:, pl.ds(k * 128, 128)].astype(jnp.float32)
        folded += piece * piece
    norms[...] = jnp.sum(folded.T, axis=0, keepdims=True)

    def from_line(zz, onward, has_onward):
        idx = at(zz, y, core)
        arrived(idx)
        pl.when(has_onward)(lambda: outgoing(idx, out.at[idx], onward).start())
        for k in range(len(sides)):
            outgoing(idx, out.at[idx], "side", k).start()
        outgoing(idx, out.at[idx], "twin").start()

    def from_side(zz):
        for other in sides:
            idx = at(zz, other, core)
            arrived(idx)
            outgoing(idx, out.at[idx], "twin").start()

    for d in range(1, depth + 1):
        if d < depth:
            pl.when(z - d >= 0)(functools.partial(from_line, z - d, "up", has_up))
            pl.when(z + d < depth)(functools.partial(from_line, z + d, "down", has_down))
        if d == 1:
            from_side(z)
        else:
            pl.when(z - d + 1 >= 0)(functools.partial(from_side, z - d + 1))
            pl.when(z + d - 1 < depth)(functools.partial(from_side, z + d - 1))

    for zz in range(depth):
        for yy in range(width):
            arrived(at(zz, yy, 1 - core))

    keep.wait()
    for zz in range(depth):
        idx = at(zz, y, core)
        pl.when(has_up & (zz <= z))(lambda: outgoing(idx, mine, "up").wait_send())
        pl.when(has_down & (zz >= z))(lambda: outgoing(idx, mine, "down").wait_send())
        for k in range(len(sides)):
            outgoing(idx, mine, "side", k).wait_send()
        for yy in range(width):
            outgoing(at(zz, yy, core), mine, "twin").wait_send()


def gather_blocks(turned, references, width):
    count = lax.axis_size("orient")
    depth = count // (2 * width)
    return pl.pallas_call(
        functools.partial(gather_kernel, depth, width),
        in_specs=[pl.BlockSpec(memory_space=pltpu.VMEM)] * 2,
        out_specs=[pl.BlockSpec(memory_space=pl.ANY), pl.BlockSpec(memory_space=pltpu.VMEM)],
        out_shape=[
            jax.ShapeDtypeStruct((count,) + turned.shape, turned.dtype),
            jax.ShapeDtypeStruct((1, TILE), jnp.float32),
        ],
        scratch_shapes=[
            pltpu.SemaphoreType.DMA((count,)),
            pltpu.SemaphoreType.DMA((count,)),
            pltpu.SemaphoreType.DMA((max(width - 1, 1), count)),
            pltpu.SemaphoreType.DMA((count,)),
            pltpu.SemaphoreType.DMA((count,)),
            pltpu.SemaphoreType.DMA,
        ],
        compiler_params=pltpu.CompilerParams(collective_id=0, has_side_effects=True),
        name="gather",
    )(turned, references)


def merge_kernel(count, mine, top, total, evidence, landed, send_sem, recv_sem):
    me = lax.axis_index("orient")
    others = [lax.rem(me + k, count) for k in range(1, count)]
    greet([(other, me >= 0) for other in others])
    copies = [
        remote(mine, landed.at[k], send_sem.at[k], recv_sem.at[k], other)
        for k, other in enumerate(others)
    ]
    for copy in copies:
        copy.start()
    for copy in copies:
        copy.wait_recv()
    half = mine.shape[0] // 2
    best = mine[:half]
    for k in range(count - 1):
        best = jnp.maximum(best, landed[k, :half])
    joint = mine[half:] * jnp.exp(mine[:half] - best)
    for k in range(count - 1):
        joint += landed[k, half:] * jnp.exp(landed[k, :half] - best)
    top[...] = best
    total[...] = joint
    evidence[...] = best + jnp.log(joint)
    for copy in copies:
        copy.wait_send()


def merge_stats(stats):
    count = lax.axis_size("orient")
    half = jax.ShapeDtypeStruct((stats.shape[0] // 2, TILE), jnp.float32)
    vmem = pl.BlockSpec(memory_space=pltpu.VMEM)
    return pl.pallas_call(
        functools.partial(merge_kernel, count),
        in_specs=[vmem],
        out_specs=[vmem] * 3,
        out_shape=[half] * 3,
        scratch_shapes=[
            pltpu.VMEM((count - 1,) + stats.shape, jnp.float32),
            pltpu.SemaphoreType.DMA((count - 1,)),
            pltpu.SemaphoreType.DMA((count - 1,)),
        ],
        compiler_params=pltpu.CompilerParams(collective_id=1, has_side_effects=True),
        name="merge",
    )(stats)


def score_kernel(
    blocks, starts, count, me, images, refs, norms, cos_ref, sin_ref,
    shifted, scores, stats, best, wide,
):
    slot, part = pl.program_id(0), pl.program_id(1)
    half = K // 2

    @pl.when((slot == 0) & (part == 0))
    def _():
        row = lax.broadcasted_iota(jnp.int32, stats.shape, 0)
        stats[...] = jnp.where(row < stats.shape[0] // 2, very_negative, 0.0)

    @pl.when((slot < count[me[0]]) & (part == 0))
    def _():
        wide[...] = images[...].astype(jnp.float32).reshape(TILE, K)

    @pl.when(slot < count[me[0]])
    def _():
        tallest = None
        for first in range(0, SHIFTS, MERGED):
            for t in range(first, first + MERGED):
                g = starts[slot, me[0]] + part * SHIFTS + t
                real, imag = wide[:, :half], wide[:, half:]
                c = cos_ref[pl.ds(g, 1), :]
                s = sin_ref[pl.ds(g, 1), :]
                rows = pl.ds(t * TILE, TILE)
                shifted[rows, :half] = (real * c - imag * s).astype(jnp.bfloat16)
                shifted[rows, half:] = (real * s + imag * c).astype(jnp.bfloat16)
            rows = pl.ds(first * TILE, MERGED * TILE)
            products = lax.dot_general(
                shifted[rows, :], refs[...], (((1,), (1,)), ((), ())),
                preferred_element_type=jnp.float32,
            )
            values = (products - 0.5 * norms[...]) * (1.0 / math.sqrt(K))
            scores[part, rows, :] = values
            highest = jnp.max(values.reshape(MERGED, TILE, TILE), axis=0)
            tallest = highest if first == 0 else jnp.maximum(tallest, highest)

        @pl.when(part == 0)
        def _():
            best[...] = tallest

        @pl.when(part > 0)
        def _():
            best[...] = jnp.maximum(best[...], tallest)

        @pl.when(part == NSH // SHIFTS - 1)
        def _():
            top = jnp.max(best[...], axis=1, keepdims=True)
            total = jnp.zeros((TILE, TILE), jnp.float32)
            for q in range(NSH // SHIFTS):
                for t in range(SHIFTS):
                    total += jnp.exp(scores[q, pl.ds(t * TILE, TILE), :] - top)
            block = blocks[slot, me[0]]
            stats[pl.ds(block, 1), :] = jnp.max(best[...].T, axis=0, keepdims=True)
            stats[pl.ds(block + stats.shape[0] // 2, 1), :] = jnp.sum(
                total.T, axis=0, keepdims=True
            )


def update_kernel(blocks, count, me, shifted, scores, tops, sums, update, mass):
    slot, part = pl.program_id(0), pl.program_id(1)

    @pl.when((slot == 0) & (part == 0))
    def _():
        update[...] = jnp.zeros_like(update)
        mass[...] = jnp.zeros_like(mass)

    @pl.when(slot < count[me[0]])
    def _():
        row = pl.ds(blocks[slot, me[0]], 1)
        top = jnp.broadcast_to(tops[row, :], (TILE, TILE)).T
        total = jnp.broadcast_to(sums[row, :], (TILE, TILE)).T
        values = scores[...].reshape(FOLD, TILE, TILE)
        weights = (jnp.exp(values - top[None]) / total[None]).astype(jnp.bfloat16)
        weights = weights.reshape(FOLD * TILE, TILE)
        mass[...] += jnp.sum(weights.astype(jnp.float32), axis=0, keepdims=True)
        update[...] += lax.dot_general(
            weights, shifted[...], (((0,), (0,)), ((), ())),
            preferred_element_type=jnp.float32,
        )


def held(slot, count, me):
    return jnp.minimum(slot, count[me[0]] - 1)


def held_part(slot, part, count, me, parts):
    return jnp.where(slot < count[me[0]], part, parts - 1)


def whole(shape):
    return pl.BlockSpec(shape, lambda s, p, *_: (0,) * len(shape))


def run_scores(blocks, starts, count, me, by_block, references, norms, cos_table, sin_table):
    most, parts = blocks.shape[0], NSH // SHIFTS
    block_total = by_block.shape[1]
    lead, _, deep, _ = by_block.shape
    return pl.pallas_call(
        score_kernel,
        grid_spec=pltpu.PrefetchScalarGridSpec(
            num_scalar_prefetch=4,
            grid=(most, parts),
            in_specs=[
                pl.BlockSpec(
                    (lead, None, deep, K),
                    lambda s, p, b, g, c, i: (0, b[held(s, c, i), i[0]], 0, 0),
                ),
                whole((TILE, K)),
                whole((1, TILE)),
                whole((GRID, K // 2)),
                whole((GRID, K // 2)),
            ],
            out_specs=[
                pl.BlockSpec(
                    (None, SHIFTS * TILE, K),
                    lambda s, p, b, g, c, i: (held(s, c, i), held_part(s, p, c, i, parts), 0),
                ),
                pl.BlockSpec(
                    (None, parts, SHIFTS * TILE, TILE),
                    lambda s, p, b, g, c, i: (held(s, c, i), 0, 0, 0),
                ),
                whole((2 * block_total, TILE)),
            ],
            scratch_shapes=[
                pltpu.VMEM((TILE, TILE), jnp.float32),
                pltpu.VMEM((TILE, K), jnp.float32),
            ],
        ),
        out_shape=[
            jax.ShapeDtypeStruct((most, NSH * TILE, K), jnp.bfloat16),
            jax.ShapeDtypeStruct((most, parts, SHIFTS * TILE, TILE), jnp.float32),
            jax.ShapeDtypeStruct((2 * block_total, TILE), jnp.float32),
        ],
        name="scores",
    )(blocks, starts, count, me, by_block, references, norms, cos_table, sin_table)


def run_update(blocks, count, me, shifted, scores, tops, sums):
    most, parts = blocks.shape[0], NSH // FOLD
    block_total = tops.shape[0]
    scores = scores.reshape(most, NSH * TILE, TILE)
    return pl.pallas_call(
        update_kernel,
        grid_spec=pltpu.PrefetchScalarGridSpec(
            num_scalar_prefetch=3,
            grid=(most, parts),
            in_specs=[
                pl.BlockSpec(
                    (None, FOLD * TILE, K),
                    lambda s, p, b, c, i: (held(s, c, i), held_part(s, p, c, i, parts), 0),
                ),
                pl.BlockSpec(
                    (None, FOLD * TILE, TILE),
                    lambda s, p, b, c, i: (held(s, c, i), held_part(s, p, c, i, parts), 0),
                ),
                whole((block_total, TILE)),
                whole((block_total, TILE)),
            ],
            out_specs=[whole((TILE, K)), whole((1, TILE))],
        ),
        out_shape=[
            jax.ShapeDtypeStruct((TILE, K), jnp.float32),
            jax.ShapeDtypeStruct((1, TILE), jnp.float32),
        ],
        name="update",
    )(blocks, count, me, shifted, scores, tops, sums)


def body(width, particles, references, tile_blocks, tile_count, shift_start):
    local_rows = particles.shape[0]
    axis_count = lax.axis_size("orient")
    my_index = lax.axis_index("orient")
    total_rows = local_rows * axis_count
    block_total = total_rows // TILE
    per = local_rows // block_total
    blocks, starts = tile_blocks.T, shift_start.T
    me = my_index.reshape(1)
    cos_table, sin_table = phase_tables()

    turned = particles.reshape(per, block_total, K).transpose(1, 0, 2)
    by_block, norms = gather_blocks(turned, references, width)
    if per % 8:
        by_block = by_block.transpose(1, 0, 2, 3).reshape(1, block_total, TILE, K)

    shifted, scores, stats = run_scores(
        blocks, starts, tile_count, me, by_block, references, norms, cos_table, sin_table
    )
    global_top, global_sum, evidence = merge_stats(stats)

    update, mass = run_update(blocks, tile_count, me, shifted, scores, global_top, global_sum)
    mine = lax.dynamic_slice_in_dim(evidence, my_index * per, per, 1)
    return update, mass.reshape(TILE), mine.T.reshape(local_rows)


def solution(mesh):
    in_specs = (
        P(("grp", "orient"), None),
        P(("grp", "orient"), None),
        P("grp", None),
        P("grp"),
        P("grp", None),
    )
    out_specs = (P(("grp", "orient"), None), P(("grp", "orient")), P(("grp", "orient")))
    width = max(1, 4 // mesh.shape["grp"])
    if mesh.shape["orient"] % (2 * width):
        width = 1
    return jax.shard_map(functools.partial(body, width), mesh=mesh, in_specs=in_specs, out_specs=out_specs, check_vma=False)
```

```python
import functools
import math

import jax
import jax.numpy as jnp
from jax import lax
from jax.experimental import pallas as pl
from jax.experimental.pallas import tpu as pltpu
from jax.sharding import PartitionSpec as P

K = 2048
NSH = 16
TILE = 128
GRID = 2 * NSH
SHIFTS = 16
MERGED = 4
FOLD = 16
PIECES = 2

very_negative = -1e30


def phase_tables():
    half_width = K // 2
    freq_index = jnp.arange(half_width, dtype=jnp.int32)
    freq_x = (freq_index % 32).astype(jnp.float32)
    freq_y = (freq_index // 32 - K // 128).astype(jnp.float32)
    grid_index = jnp.arange(GRID, dtype=jnp.int32)
    delta_x = (grid_index - 16).astype(jnp.float32) * 0.5
    delta_y = (5 * grid_index % 7 - 3).astype(jnp.float32) * 0.5
    angles = (
        2.0
        * math.pi
        / 64.0
        * (delta_x[:, None] * freq_x[None, :] + delta_y[:, None] * freq_y[None, :])
    )
    return jnp.cos(angles), jnp.sin(angles)


def remote(src, dst, send, recv, target):
    return pltpu.make_async_remote_copy(
        src_ref=src,
        dst_ref=dst,
        send_sem=send,
        recv_sem=recv,
        device_id={"orient": target},
        device_id_type=pl.DeviceIdType.MESH,
    )


def greet(neighbours):
    barrier = pltpu.get_barrier_semaphore()
    arrivals = 0
    for target, present in neighbours:

        @pl.when(present)
        def _():
            pl.semaphore_signal(
                barrier, inc=1, device_id={"orient": target},
                device_id_type=pl.DeviceIdType.MESH,
            )

        arrivals = arrivals + jnp.where(present, 1, 0)
    pl.semaphore_wait(barrier, arrivals)


def gather_kernel(
    depth, width, mine, refs, out, norms, up_sem, down_sem, side_sem, twin_sem, recv_sem, own_sem
):
    me = lax.axis_index("orient")
    core = lax.rem(me, 2)
    chip = me // 2
    z, y = chip // width, lax.rem(chip, width)

    def at(zz, yy, cc):
        return (zz * width + yy) * 2 + cc

    up, down, twin = at(z + 1, y, core), at(z - 1, y, core), at(z, y, 1 - core)
    sides = [lax.rem(y + k, width) for k in range(1, width)]
    has_up, has_down = z < depth - 1, z > 0
    greet(
        [(up, has_up), (down, has_down), (twin, me >= 0)]
        + [(at(z, other, core), me >= 0) for other in sides]
    )

    cut = mine.shape[0] // PIECES

    def outgoing(idx, src, kind, h, k=0):
        send, target = dict(
            up=(up_sem, up),
            down=(down_sem, down),
            twin=(twin_sem, twin),
            side=(side_sem.at[k], at(z, sides[k], core) if sides else me),
        )[kind]
        piece = pl.ds(h * cut, cut)
        spot = idx * PIECES + h
        return remote(
            src.at[piece], out.at[idx, piece], send.at[spot], recv_sem.at[spot], target
        )

    def arrived(idx, h):
        outgoing(idx, out.at[idx], "twin", h).wait_recv()

    for h in range(PIECES):
        pl.when(has_up)(lambda: outgoing(me, mine, "up", h).start())
        pl.when(has_down)(lambda: outgoing(me, mine, "down", h).start())
        for k in range(len(sides)):
            outgoing(me, mine, "side", h, k).start()
        outgoing(me, mine, "twin", h).start()
    keep = pltpu.make_async_copy(mine, out.at[me], own_sem)
    keep.start()

    folded = jnp.zeros((TILE, 128), jnp.float32)
    for k in range(K // 128):
        piece = refs[:, pl.ds(k * 128, 128)].astype(jnp.float32)
        folded += piece * piece
    norms[...] = jnp.sum(folded.T, axis=0, keepdims=True)

    def from_line(zz, onward, has_onward, h):
        idx = at(zz, y, core)
        arrived(idx, h)
        pl.when(has_onward)(lambda: outgoing(idx, out.at[idx], onward, h).start())
        for k in range(len(sides)):
            outgoing(idx, out.at[idx], "side", h, k).start()
        outgoing(idx, out.at[idx], "twin", h).start()

    def from_side(zz, h):
        for other in sides:
            idx = at(zz, other, core)
            arrived(idx, h)
            outgoing(idx, out.at[idx], "twin", h).start()

    for d in range(1, depth + 1):
        for h in range(PIECES):
            if d < depth:
                pl.when(z - d >= 0)(functools.partial(from_line, z - d, "up", has_up, h))
                pl.when(z + d < depth)(functools.partial(from_line, z + d, "down", has_down, h))
            if d == 1:
                from_side(z, h)
            else:
                pl.when(z - d + 1 >= 0)(functools.partial(from_side, z - d + 1, h))
                pl.when(z + d - 1 < depth)(functools.partial(from_side, z + d - 1, h))

    for zz in range(depth):
        for yy in range(width):
            for h in range(PIECES):
                arrived(at(zz, yy, 1 - core), h)

    keep.wait()
    for zz in range(depth):
        idx = at(zz, y, core)
        for h in range(PIECES):
            pl.when(has_up & (zz <= z))(lambda: outgoing(idx, mine, "up", h).wait_send())
            pl.when(has_down & (zz >= z))(lambda: outgoing(idx, mine, "down", h).wait_send())
            for k in range(len(sides)):
                outgoing(idx, mine, "side", h, k).wait_send()
            for yy in range(width):
                outgoing(at(zz, yy, core), mine, "twin", h).wait_send()


def gather_blocks(turned, references, width):
    count = lax.axis_size("orient")
    depth = count // (2 * width)
    return pl.pallas_call(
        functools.partial(gather_kernel, depth, width),
        in_specs=[pl.BlockSpec(memory_space=pltpu.VMEM)] * 2,
        out_specs=[pl.BlockSpec(memory_space=pl.ANY), pl.BlockSpec(memory_space=pltpu.VMEM)],
        out_shape=[
            jax.ShapeDtypeStruct((count,) + turned.shape, turned.dtype),
            jax.ShapeDtypeStruct((1, TILE), jnp.float32),
        ],
        scratch_shapes=[
            pltpu.SemaphoreType.DMA((PIECES * count,)),
            pltpu.SemaphoreType.DMA((PIECES * count,)),
            pltpu.SemaphoreType.DMA((max(width - 1, 1), PIECES * count)),
            pltpu.SemaphoreType.DMA((PIECES * count,)),
            pltpu.SemaphoreType.DMA((PIECES * count,)),
            pltpu.SemaphoreType.DMA,
        ],
        compiler_params=pltpu.CompilerParams(collective_id=0, has_side_effects=True),
        name="gather",
    )(turned, references)


def merge_kernel(count, mine, top, total, evidence, landed, send_sem, recv_sem):
    me = lax.axis_index("orient")
    others = [lax.rem(me + k, count) for k in range(1, count)]
    greet([(other, me >= 0) for other in others])
    copies = [
        remote(mine, landed.at[k], send_sem.at[k], recv_sem.at[k], other)
        for k, other in enumerate(others)
    ]
    for copy in copies:
        copy.start()
    for copy in copies:
        copy.wait_recv()
    half = mine.shape[0] // 2
    best = mine[:half]
    for k in range(count - 1):
        best = jnp.maximum(best, landed[k, :half])
    joint = mine[half:] * jnp.exp(mine[:half] - best)
    for k in range(count - 1):
        joint += landed[k, half:] * jnp.exp(landed[k, :half] - best)
    top[...] = best
    total[...] = joint
    evidence[...] = best + jnp.log(joint)
    for copy in copies:
        copy.wait_send()


def merge_stats(stats):
    count = lax.axis_size("orient")
    half = jax.ShapeDtypeStruct((stats.shape[0] // 2, TILE), jnp.float32)
    vmem = pl.BlockSpec(memory_space=pltpu.VMEM)
    return pl.pallas_call(
        functools.partial(merge_kernel, count),
        in_specs=[vmem],
        out_specs=[vmem] * 3,
        out_shape=[half] * 3,
        scratch_shapes=[
            pltpu.VMEM((count - 1,) + stats.shape, jnp.float32),
            pltpu.SemaphoreType.DMA((count - 1,)),
            pltpu.SemaphoreType.DMA((count - 1,)),
        ],
        compiler_params=pltpu.CompilerParams(collective_id=1, has_side_effects=True),
        name="merge",
    )(stats)


def score_kernel(
    blocks, starts, count, me, images, refs, norms, cos_ref, sin_ref,
    shifted, scores, stats, best, wide,
):
    slot, part = pl.program_id(0), pl.program_id(1)
    half = K // 2

    @pl.when((slot == 0) & (part == 0))
    def _():
        row = lax.broadcasted_iota(jnp.int32, stats.shape, 0)
        stats[...] = jnp.where(row < stats.shape[0] // 2, very_negative, 0.0)

    @pl.when((slot < count[me[0]]) & (part == 0))
    def _():
        wide[...] = images[...].astype(jnp.float32).reshape(TILE, K)

    @pl.when(slot < count[me[0]])
    def _():
        tallest = None
        for first in range(0, SHIFTS, MERGED):
            for t in range(first, first + MERGED):
                g = starts[slot, me[0]] + part * SHIFTS + t
                real, imag = wide[:, :half], wide[:, half:]
                c = cos_ref[pl.ds(g, 1), :]
                s = sin_ref[pl.ds(g, 1), :]
                rows = pl.ds(t * TILE, TILE)
                shifted[rows, :half] = (real * c - imag * s).astype(jnp.bfloat16)
                shifted[rows, half:] = (real * s + imag * c).astype(jnp.bfloat16)
            rows = pl.ds(first * TILE, MERGED * TILE)
            products = lax.dot_general(
                shifted[rows, :], refs[...], (((1,), (1,)), ((), ())),
                preferred_element_type=jnp.float32,
            )
            values = (products - 0.5 * norms[...]) * (1.0 / math.sqrt(K))
            scores[part, rows, :] = values
            highest = jnp.max(values.reshape(MERGED, TILE, TILE), axis=0)
            tallest = highest if first == 0 else jnp.maximum(tallest, highest)

        @pl.when(part == 0)
        def _():
            best[...] = tallest

        @pl.when(part > 0)
        def _():
            best[...] = jnp.maximum(best[...], tallest)

        @pl.when(part == NSH // SHIFTS - 1)
        def _():
            top = jnp.max(best[...], axis=1, keepdims=True)
            total = jnp.zeros((TILE, TILE), jnp.float32)
            for q in range(NSH // SHIFTS):
                for t in range(SHIFTS):
                    total += jnp.exp(scores[q, pl.ds(t * TILE, TILE), :] - top)
            block = blocks[slot, me[0]]
            stats[pl.ds(block, 1), :] = jnp.max(best[...].T, axis=0, keepdims=True)
            stats[pl.ds(block + stats.shape[0] // 2, 1), :] = jnp.sum(
                total.T, axis=0, keepdims=True
            )


def update_kernel(blocks, count, me, shifted, scores, tops, sums, update, mass):
    slot, part = pl.program_id(0), pl.program_id(1)

    @pl.when((slot == 0) & (part == 0))
    def _():
        update[...] = jnp.zeros_like(update)
        mass[...] = jnp.zeros_like(mass)

    @pl.when(slot < count[me[0]])
    def _():
        row = pl.ds(blocks[slot, me[0]], 1)
        top = jnp.broadcast_to(tops[row, :], (TILE, TILE)).T
        total = jnp.broadcast_to(sums[row, :], (TILE, TILE)).T
        values = scores[...].reshape(FOLD, TILE, TILE)
        weights = (jnp.exp(values - top[None]) / total[None]).astype(jnp.bfloat16)
        weights = weights.reshape(FOLD * TILE, TILE)
        mass[...] += jnp.sum(weights.astype(jnp.float32), axis=0, keepdims=True)
        update[...] += lax.dot_general(
            weights, shifted[...], (((0,), (0,)), ((), ())),
            preferred_element_type=jnp.float32,
        )


def held(slot, count, me):
    return jnp.minimum(slot, count[me[0]] - 1)


def held_part(slot, part, count, me, parts):
    return jnp.where(slot < count[me[0]], part, parts - 1)


def whole(shape):
    return pl.BlockSpec(shape, lambda s, p, *_: (0,) * len(shape))


def run_scores(blocks, starts, count, me, by_block, references, norms, cos_table, sin_table):
    most, parts = blocks.shape[0], NSH // SHIFTS
    block_total = by_block.shape[1]
    lead, _, deep, _ = by_block.shape
    return pl.pallas_call(
        score_kernel,
        grid_spec=pltpu.PrefetchScalarGridSpec(
            num_scalar_prefetch=4,
            grid=(most, parts),
            in_specs=[
                pl.BlockSpec(
                    (lead, None, deep, K),
                    lambda s, p, b, g, c, i: (0, b[held(s, c, i), i[0]], 0, 0),
                ),
                whole((TILE, K)),
                whole((1, TILE)),
                whole((GRID, K // 2)),
                whole((GRID, K // 2)),
            ],
            out_specs=[
                pl.BlockSpec(
                    (None, SHIFTS * TILE, K),
                    lambda s, p, b, g, c, i: (held(s, c, i), held_part(s, p, c, i, parts), 0),
                ),
                pl.BlockSpec(
                    (None, parts, SHIFTS * TILE, TILE),
                    lambda s, p, b, g, c, i: (held(s, c, i), 0, 0, 0),
                ),
                whole((2 * block_total, TILE)),
            ],
            scratch_shapes=[
                pltpu.VMEM((TILE, TILE), jnp.float32),
                pltpu.VMEM((TILE, K), jnp.float32),
            ],
        ),
        out_shape=[
            jax.ShapeDtypeStruct((most, NSH * TILE, K), jnp.bfloat16),
            jax.ShapeDtypeStruct((most, parts, SHIFTS * TILE, TILE), jnp.float32),
            jax.ShapeDtypeStruct((2 * block_total, TILE), jnp.float32),
        ],
        name="scores",
    )(blocks, starts, count, me, by_block, references, norms, cos_table, sin_table)


def run_update(blocks, count, me, shifted, scores, tops, sums):
    most, parts = blocks.shape[0], NSH // FOLD
    block_total = tops.shape[0]
    scores = scores.reshape(most, NSH * TILE, TILE)
    return pl.pallas_call(
        update_kernel,
        grid_spec=pltpu.PrefetchScalarGridSpec(
            num_scalar_prefetch=3,
            grid=(most, parts),
            in_specs=[
                pl.BlockSpec(
                    (None, FOLD * TILE, K),
                    lambda s, p, b, c, i: (held(s, c, i), held_part(s, p, c, i, parts), 0),
                ),
                pl.BlockSpec(
                    (None, FOLD * TILE, TILE),
                    lambda s, p, b, c, i: (held(s, c, i), held_part(s, p, c, i, parts), 0),
                ),
                whole((block_total, TILE)),
                whole((block_total, TILE)),
            ],
            out_specs=[whole((TILE, K)), whole((1, TILE))],
        ),
        out_shape=[
            jax.ShapeDtypeStruct((TILE, K), jnp.float32),
            jax.ShapeDtypeStruct((1, TILE), jnp.float32),
        ],
        name="update",
    )(blocks, count, me, shifted, scores, tops, sums)


def body(width, particles, references, tile_blocks, tile_count, shift_start):
    local_rows = particles.shape[0]
    axis_count = lax.axis_size("orient")
    my_index = lax.axis_index("orient")
    total_rows = local_rows * axis_count
    block_total = total_rows // TILE
    per = local_rows // block_total
    blocks, starts = tile_blocks.T, shift_start.T
    me = my_index.reshape(1)
    cos_table, sin_table = phase_tables()

    turned = particles.reshape(per, block_total, K).transpose(1, 0, 2)
    by_block, norms = gather_blocks(turned, references, width)
    if per % 8:
        by_block = by_block.transpose(1, 0, 2, 3).reshape(1, block_total, TILE, K)

    shifted, scores, stats = run_scores(
        blocks, starts, tile_count, me, by_block, references, norms, cos_table, sin_table
    )
    global_top, global_sum, evidence = merge_stats(stats)

    update, mass = run_update(blocks, tile_count, me, shifted, scores, global_top, global_sum)
    mine = lax.dynamic_slice_in_dim(evidence, my_index * per, per, 1)
    return update, mass.reshape(TILE), mine.T.reshape(local_rows)


def solution(mesh):
    in_specs = (
        P(("grp", "orient"), None),
        P(("grp", "orient"), None),
        P("grp", None),
        P("grp"),
        P("grp", None),
    )
    out_specs = (P(("grp", "orient"), None), P(("grp", "orient")), P(("grp", "orient")))
    width = max(1, 4 // mesh.shape["grp"])
    if mesh.shape["orient"] % (2 * width):
        width = 1
    return jax.shard_map(functools.partial(body, width), mesh=mesh, in_specs=in_specs, out_specs=out_specs, check_vma=False)
```
